32 devices in a mesh: groups: 2 (over y), expert: 4 (over z), dp: 2 (over x), inner: 2 (over core).
Axes of the slice: x: 2, y: 2, z: 4, core: 2. Of those that a mesh axis runs over, the one named last changes fastest.
Arguments:
- tokens: bfloat16 [2048, 2048], P(('groups', 'expert', 'inner'), 'dp'), parts along dimension 0, may hold values from -6 to 6
- out_grad: bfloat16 [2048, 2048], P(('groups', 'expert', 'inner'), 'dp'), parts along dimension 0, may hold values from -2.5 to 2.5
- expert_ids: int32 [2048, 2], P(('groups', 'expert', 'inner')), parts along dimension 0, may hold values from 0 to 7, all different within a row; in each aligned block of 128 rows (0 to 127, 128 to 255, ...) at most 48 rows name the same one
- gate_weights: float32 [2048, 2], P(('groups', 'expert', 'inner')), parts along dimension 0, may hold values from 0.2 to 1
- shadow_expert: int32 [4], replicated, may hold values from 0 to 7, as said below
- w_gate: bfloat16 [8, 2048, 1024], P('expert', 'dp', 'inner'), may hold values from -0.125 to 0.125
- w_up: bfloat16 [8, 2048, 1024], P('expert', 'dp', 'inner'), may hold values from -0.125 to 0.125
- w_down: bfloat16 [8, 1024, 2048], P('expert', 'inner', 'dp'), may hold values from -0.1875 to 0.1875
- copy_gate: bfloat16 [4, 2048, 1024], P('expert', 'dp', 'inner'), may hold values from -0.125 to 0.125
- copy_up: bfloat16 [4, 2048, 1024], P('expert', 'dp', 'inner'), may hold values from -0.125 to 0.125
- copy_down: bfloat16 [4, 1024, 2048], P('expert', 'inner', 'dp'), may hold values from -0.1875 to 0.1875
Outputs:
- grad_tokens: bfloat16 [2048, 2048], P(('groups', 'expert', 'inner'), 'dp'), parts along dimension 0
- grad_w_gate: bfloat16 [16, 2048, 1024], P(('groups', 'expert'), 'dp', 'inner'), parts along dimension 0
- grad_w_up: bfloat16 [16, 2048, 1024], P(('groups', 'expert'), 'dp', 'inner'), parts along dimension 0
- grad_w_down: bfloat16 [16, 1024, 2048], P(('groups', 'expert'), 'inner', 'dp'), parts along dimension 0
The draws below stay inside these ranges and needn't reach their ends.
There are 2 independent parts, one for each index of `groups`. The reference program is written for one: setup_inputs(seed, part) draws one part's arguments, and reference() takes and returns one part's arrays. A program takes and returns all parts, laid end to end along the dimension named above; an argument that names none is the same for every part. Nothing has to cross between parts.
Inputs may be any that keep to these rules, and one draw needn't show every extreme that they name: `expert_ids`: A token's two experts differ; among the 128 tokens of one index of expert+inner no expert is named more than 48 times, a bound that some block reaches. Experts 2 j and 2 j + 1 are owned by index j of expert. `shadow_expert`: entry j names an expert that index j does not own. Exactly half of the indices of expert own the experts of two entries each, the other indices those of none; the two entries that fall on one index may name the same expert or its two experts.
All inputs are finite; a program needn't handle non-finite values.
Results may differ from the reference program's by a relative error of at most 0.02.
Values may be sent and summed in bfloat16 or wider, within the bound.
A program may use at most 128 MiB of HBM per device.

```python
import math
import jax
import jax.numpy as jnp
import numpy as np
from jax import lax

D = 2048
H = 1024
TOK_DEV = 128
TOKENS = 1024
EXPERTS = 8
MOST = 48
N_EXPERT = 4
N_DP = 2


def draw_shadow_expert(key, part):
    first_key, second_key = jax.random.split(jax.random.fold_in(key, 17))
    order = jax.random.permutation(first_key, N_EXPERT).astype(jnp.int32)
    position = jnp.arange(N_EXPERT, dtype=jnp.int32)
    owner_by_position = order[(2 * (position // 2) + 2) % N_EXPERT]
    target = jnp.zeros((N_EXPERT,), jnp.int32).at[order].set(owner_by_position)
    member_bit = jax.random.randint(second_key, (N_EXPERT,), 0, 2)
    return (2 * target + member_bit).astype(jnp.int32)


def block_levels(rng, shape, cuts, least, largest):
    def one(dim, parts):
        draws = jax.random.uniform(jax.random.fold_in(jax.random.fold_in(rng, 6), dim), (parts,), jnp.float32, least / len(cuts), largest / len(cuts))
        return jnp.repeat(jnp.exp(draws), shape[dim] // parts).reshape((-1,) + (1,) * (len(shape) - dim - 1))

    factor_of = one(*cuts[0])
    for cut in cuts[1:]:
        factor_of = factor_of * one(*cut)
    return factor_of


def assign_block(key, own, number, rows, count, top, most, skew):
    ranking = jax.random.permutation(key, count)
    heavy_load, usual = portions_of(count, rows * top, most, skew, True), portions_of(count, rows * top, most, skew, False)
    places = jnp.arange(count)

    def named(tallies, turn):
        used = int((tallies > 0).sum())
        fixed = max(1, used // 4)
        moved = fixed + (places - fixed + turn * (used - fixed)) % max(1, count - fixed)
        return jnp.zeros((count,), jnp.int32).at[ranking[jnp.where(places < fixed, places, moved)]].set(jnp.asarray(tallies, jnp.int32))

    tallies = jnp.where(number % 4 == 0, named(heavy_load, number // 4), named(usual, number - number // 4 - 1))
    mixed = jax.random.permutation(jax.random.fold_in(own, 3), count)
    source_of, taker = mixed[0:count // 2 * 2:2], mixed[1:count // 2 * 2:2]
    room = jnp.minimum(tallies[source_of] - 1, most - tallies[taker]) // 2
    room = jnp.where((source_of == ranking[0]) | (taker == ranking[0]) | (tallies[taker] == 0), 0, jnp.maximum(room, 0))
    moved = jax.random.randint(jax.random.fold_in(own, 4), (count // 2,), 0, 1 << 20) % (room + 1)
    tallies = tallies.at[source_of].add(-moved).at[taker].add(moved)
    items = jnp.searchsorted(jnp.cumsum(tallies), jnp.arange(rows * top), side="right").astype(jnp.int32)
    table = items.reshape(top, rows).T
    table = table[jax.random.permutation(jax.random.fold_in(own, 1), rows)]
    turn = jax.random.randint(jax.random.fold_in(own, 2), (rows, 1), 0, top)
    return jnp.take_along_axis(table, (jnp.arange(top)[None, :] + turn) % top, axis=1)


def portions_of(amount, total, bound, lean, full):
    weights = [(1 << 20) // math.isqrt(standing ** lean) + 1 for standing in range(1, amount + 1)]
    largest = bound if full else min(bound, max(-(-total // amount), total * weights[0] // sum(weights)))
    least = 1 if total - largest >= amount - 1 else 0
    given, surplus = [largest] + [least] * (amount - 1), total - largest - least * (amount - 1)
    while surplus > 0:
        candidates = [i for i in range(1, amount) if given[i] < largest] or [i for i in range(1, amount) if given[i] < bound]
        mass, budget = sum([weights[i] for i in candidates]), surplus
        for i in candidates:
            extra = min(bound - given[i], max(1, budget * weights[i] // mass), surplus)
            given[i] = given[i] + extra
            surplus = surplus - extra
    return np.array(given)


def noise(key, shape, spread, limit, shards=(), held_as=jnp.bfloat16):
    array = jax.random.normal(key, shape, jnp.float32) * spread
    if len(shards) > 0:
        array = block_levels(key, shape, shards, -0.22, 0.18) * array
    return jnp.clip(array, min=-limit, max=limit).astype(held_as)


def setup_inputs(seed: int = 0, part: int = 0) -> dict:
    arg_keys = jax.random.split(jax.random.key(seed), 12)
    own_keys = jax.random.split(jax.random.fold_in(arg_keys[11], part), 12)
    tokens = noise(own_keys[0], (TOKENS, D), 1.0, 6.0, ((0, 8), (1, 2)))
    out_grad = noise(own_keys[1], (TOKENS, D), 0.3, 2.5, ((0, 8), (1, 2)))
    expert_ids_keys = jax.random.split(jax.random.fold_in(own_keys[2], 1), TOKENS // TOK_DEV)
    expert_ids_turns = jax.random.permutation(jax.random.fold_in(own_keys[2], 3), TOKENS // TOK_DEV)
    expert_ids = jax.vmap(lambda own, number: assign_block(jax.random.fold_in(own_keys[2], 2), own, number, TOK_DEV, EXPERTS, 2, MOST, 2))(expert_ids_keys, expert_ids_turns).reshape((TOKENS, 2))
    gate_weights = jnp.clip(0.2 + 0.8 * jax.random.uniform(own_keys[3], (TOKENS, 2), jnp.float32) ** block_levels(own_keys[3], (TOKENS, 2), ((0, 8),), -0.2, 0.2), 0.2, 1.0)
    shadow_expert = draw_shadow_expert(jax.random.fold_in(arg_keys[11], 71), part)
    w_gate = noise(arg_keys[5], (EXPERTS, D, H), D ** -0.5, 0.125, ((0, 4), (1, 2), (2, 2)))
    w_up = noise(arg_keys[6], (EXPERTS, D, H), D ** -0.5, 0.125, ((0, 4), (1, 2), (2, 2)))
    w_down = noise(arg_keys[7], (EXPERTS, H, D), H ** -0.5, 0.1875, ((0, 4), (1, 2), (2, 2)))
    copy_gate = noise(arg_keys[8], (N_EXPERT, D, H), D ** -0.5, 0.125, ((0, 4), (1, 2), (2, 2)))
    copy_up = noise(arg_keys[9], (N_EXPERT, D, H), D ** -0.5, 0.125, ((0, 4), (1, 2), (2, 2)))
    copy_down = noise(arg_keys[10], (N_EXPERT, H, D), H ** -0.5, 0.1875, ((0, 4), (1, 2), (2, 2)))
    return {"tokens": tokens, "out_grad": out_grad, "expert_ids": expert_ids, "gate_weights": gate_weights, "shadow_expert": shadow_expert, "w_gate": w_gate, "w_up": w_up, "w_down": w_down, "copy_gate": copy_gate, "copy_up": copy_up, "copy_down": copy_down}


def serving_copy(expert_ids, shadow_expert, first_token):
    tok_rows = expert_ids.shape[0]
    shadow_count = shadow_expert.shape[0]
    token_index = first_token + jnp.arange(tok_rows, dtype=jnp.int32)
    position = token_index[:, None] + jnp.arange(2, dtype=jnp.int32)[None, :]
    matches = (expert_ids[:, :, None] == shadow_expert[None, None, :]).astype(jnp.int32)
    copies = 1 + jnp.sum(matches, axis=2)
    chosen = position % copies
    slot_order = jnp.arange(shadow_count, dtype=jnp.int32)
    lower_slot = (slot_order[:, None] > slot_order[None, :]).astype(jnp.int32)
    same_expert = (shadow_expert[:, None] == shadow_expert[None, :]).astype(jnp.int32)
    rank_among = jnp.sum(lower_slot * same_expert, axis=1)
    picked = matches * (rank_among[None, None, :] == chosen[:, :, None] - 1).astype(jnp.int32)
    holder = jnp.sum(picked * slot_order[None, None, :], axis=2)
    shadowed = jnp.sum(picked, axis=2)
    return jnp.where(shadowed > 0, 2 * shadow_count + holder, expert_ids).astype(jnp.int32)


def activation(block_sums):
    width_half = block_sums.shape[-1] // 3
    pre_gate = block_sums[..., :width_half]
    pre_up = block_sums[..., width_half:2 * width_half]
    hidden_grad = block_sums[..., 2 * width_half:]
    sigmoid_gate = jax.nn.sigmoid(pre_gate)
    swish_gate = pre_gate * sigmoid_gate
    grad_up = (hidden_grad * swish_gate).astype(jnp.bfloat16)
    grad_gate = (hidden_grad * pre_up * sigmoid_gate * (1.0 + pre_gate * (1.0 - sigmoid_gate))).astype(jnp.bfloat16)
    hidden = (swish_gate * pre_up).astype(jnp.bfloat16)
    return grad_gate, grad_up, hidden


def settle(partial_blocks):
    rounded = lax.optimization_barrier(partial_blocks.astype(jnp.bfloat16))
    return jnp.sum(rounded.astype(jnp.float32), axis=1)


def copy_backward(inputs, grad_rows, weight_gate, weight_up, weight_down):
    row_count = inputs.shape[0]
    slice_width = D // N_DP
    split_in = inputs.astype(jnp.float32).reshape(row_count, N_DP, slice_width)
    split_grad = grad_rows.astype(jnp.float32).reshape(row_count, N_DP, slice_width)
    gate_blocks = weight_gate.astype(jnp.float32).reshape(N_DP, slice_width, H)
    up_blocks = weight_up.astype(jnp.float32).reshape(N_DP, slice_width, H)
    down_blocks = weight_down.astype(jnp.float32).reshape(H, N_DP, slice_width)
    pre_sums = jnp.concatenate([
        settle(jnp.einsum("rps,psh->rph", split_in, gate_blocks)),
        settle(jnp.einsum("rps,psh->rph", split_in, up_blocks)),
        settle(jnp.einsum("rps,hps->rph", split_grad, down_blocks))], axis=1)
    grad_gate, grad_up, hidden = activation(pre_sums)
    gate_wide = grad_gate.astype(jnp.float32)
    up_wide = grad_up.astype(jnp.float32)
    route_grad = jnp.einsum("rh,dh->rd", gate_wide, weight_gate.astype(jnp.float32)) + jnp.einsum("rh,dh->rd", up_wide, weight_up.astype(jnp.float32))
    inputs_wide = inputs.astype(jnp.float32)
    dw_gate = jnp.einsum("rd,rh->dh", inputs_wide, gate_wide)
    dw_up = jnp.einsum("rd,rh->dh", inputs_wide, up_wide)
    dw_down = jnp.einsum("rh,rd->hd", hidden.astype(jnp.float32), grad_rows.astype(jnp.float32))
    return route_grad, dw_gate, dw_up, dw_down


def reference(tokens, out_grad, expert_ids, gate_weights, shadow_expert, w_gate, w_up, w_down, copy_gate, copy_up, copy_down):
    copy_ids = serving_copy(expert_ids, shadow_expert, jnp.int32(0))
    flat_ids = copy_ids.reshape(-1)
    flat_gates = gate_weights.reshape(-1).astype(jnp.float32)
    capacity = (TOKENS // TOK_DEV) * MOST

    def gather_rows(copy_number):
        served = flat_ids == copy_number
        served_count = jnp.sum(served.astype(jnp.int32))
        route_index = jnp.nonzero(served, size=capacity, fill_value=0)[0].astype(jnp.int32)
        valid_route = (jnp.arange(capacity, dtype=jnp.int32) < served_count).astype(jnp.float32)
        token_row = route_index // 2
        inputs = tokens[token_row]
        grad_rows = ((flat_gates[route_index] * valid_route)[:, None] * out_grad[token_row].astype(jnp.float32)).astype(jnp.bfloat16)
        return token_row, inputs, grad_rows

    def shadow_step(dx_total, stacked):
        copy_number, weight_gate, weight_up, weight_down = stacked
        token_row, inputs, grad_rows = gather_rows(copy_number)
        route_grad, dw_gate, dw_up, dw_down = copy_backward(inputs, grad_rows, weight_gate, weight_up, weight_down)
        dx_total = dx_total.at[token_row].add(route_grad)
        return dx_total, (dw_gate.astype(jnp.bfloat16), dw_up.astype(jnp.bfloat16), dw_down.astype(jnp.bfloat16))

    dx_total = jnp.zeros((TOKENS, D), jnp.float32)
    shadow_numbers = EXPERTS + jnp.arange(N_EXPERT, dtype=jnp.int32)
    dx_total, panels = lax.scan(shadow_step, dx_total, (shadow_numbers, copy_gate, copy_up, copy_down))

    def owner_step(dx_total, stacked):
        copy_number, weight_gate, weight_up, weight_down = stacked
        token_row, inputs, grad_rows = gather_rows(copy_number)
        route_grad, dw_gate, dw_up, dw_down = copy_backward(inputs, grad_rows, weight_gate, weight_up, weight_down)
        dx_total = dx_total.at[token_row].add(route_grad)
        indicator = (shadow_expert == copy_number).astype(jnp.float32)
        gate_total = dw_gate + jnp.einsum("j,jdh->dh", indicator, panels[0].astype(jnp.float32))
        up_total = dw_up + jnp.einsum("j,jdh->dh", indicator, panels[1].astype(jnp.float32))
        down_total = dw_down + jnp.einsum("j,jhd->hd", indicator, panels[2].astype(jnp.float32))
        return dx_total, (gate_total.astype(jnp.bfloat16), up_total.astype(jnp.bfloat16), down_total.astype(jnp.bfloat16))

    owner_numbers = jnp.arange(EXPERTS, dtype=jnp.int32)
    dx_total, owned = lax.scan(owner_step, dx_total, (owner_numbers, w_gate, w_up, w_down))
    return (dx_total.astype(jnp.bfloat16), owned[0], owned[1], owned[2])
```

```python
import jax
import jax.numpy as jnp
from jax import lax
from jax.sharding import PartitionSpec as P

BF16 = jnp.bfloat16
F32 = jnp.float32


def serving_copy(ids, shadow_expert, token_index):
    shadow_count = shadow_expert.shape[0]
    position = token_index[None, :] + jnp.arange(2, dtype=jnp.int32)[:, None]
    matches = (ids[None] == shadow_expert[:, None, None]).astype(jnp.int32)
    copies = 1 + jnp.sum(matches, axis=0)
    chosen = position % copies
    slot_order = jnp.arange(shadow_count, dtype=jnp.int32)
    lower_slot = (slot_order[:, None] > slot_order[None, :]).astype(jnp.int32)
    same_expert = (shadow_expert[:, None] == shadow_expert[None, :]).astype(jnp.int32)
    rank_among = jnp.sum(lower_slot * same_expert, axis=1)
    picked = matches * (rank_among[:, None, None] == chosen[None] - 1).astype(jnp.int32)
    holder = jnp.sum(picked * slot_order[:, None, None], axis=0)
    shadowed = jnp.sum(picked, axis=0)
    return jnp.where(shadowed > 0, 2 * shadow_count + holder, ids)


def activation(pre_gate, pre_up, hidden_grad, served):
    sig = jax.nn.sigmoid(pre_gate)
    swish = pre_gate * sig
    grad_up = hidden_grad * swish
    grad_gate = hidden_grad * pre_up * sig * (1.0 + pre_gate * (1.0 - sig))
    hidden = swish * pre_up
    keep = served[:, None] > 0
    wide = jnp.concatenate([grad_gate, grad_up, hidden], axis=1)
    return jnp.where(keep, wide, 0.0).astype(BF16)


def mm(a, b, ca, cb):
    return lax.dot_general(a, b, (((ca,), (cb,)), ((), ())), preferred_element_type=F32)


def on_device(
    tokens,
    out_grad,
    expert_ids,
    gate_weights,
    shadow_expert,
    w_gate,
    w_up,
    w_down,
    copy_gate,
    copy_up,
    copy_down,
):
    tok_rows, features = tokens.shape
    width = w_gate.shape[2]
    expert_count = lax.axis_size("expert")
    inner_count = lax.axis_size("inner")
    dp_count = lax.axis_size("dp")
    blocks = expert_count * inner_count
    total = blocks * tok_rows
    capacity = max(2, 3 * tok_rows // (2 * expert_count))
    rows = blocks * capacity
    me = lax.axis_index("expert")
    both = ("expert", "inner")

    meta = jnp.concatenate([expert_ids.astype(F32).T, gate_weights.T], axis=0)
    meta = lax.all_gather(meta, both, axis=0, tiled=False)
    meta = jnp.transpose(meta, (1, 0, 2)).reshape(4, total)
    tokens_all = lax.all_gather(tokens, both, axis=0, tiled=True)
    grads_all = lax.all_gather(out_grad, both, axis=0, tiled=True)

    ids = meta[:2].astype(jnp.int32)
    gates = meta[2:]
    copy_ids = serving_copy(ids, shadow_expert, jnp.arange(total, dtype=jnp.int32))
    slot_expert = jnp.stack([2 * me, 2 * me + 1, shadow_expert[me]])
    slot_copy = jnp.stack([2 * me, 2 * me + 1, 2 * expert_count + me])
    member = ids[None] == slot_expert[:, None, None]
    named = jnp.sum(member.astype(F32), axis=1)
    gate_of = jnp.sum(jnp.where(member, gates[None], 0.0), axis=1)
    served_of = jnp.sum((copy_ids[None] == slot_copy[:, None, None]).astype(F32), axis=1)
    before = (jnp.arange(tok_rows)[:, None] < jnp.arange(tok_rows)[None, :]).astype(BF16)
    rank = jnp.dot(
        named.reshape(3 * blocks, tok_rows).astype(BF16), before, preferred_element_type=F32
    ).astype(jnp.int32)
    rank = rank.reshape(3, blocks, tok_rows)
    place = rank + capacity * jnp.arange(blocks, dtype=jnp.int32)[None, :, None]
    place = jnp.where(named > 0, place.reshape(3, total), -1)
    hit = place[:, None, :] == jnp.arange(rows, dtype=jnp.int32)[None, :, None]
    gate_row = jnp.sum(jnp.where(hit, gate_of[:, None, :], 0.0), axis=2)
    served_row = jnp.sum(jnp.where(hit, served_of[:, None, :], 0.0), axis=2)
    select = hit.astype(BF16)
    select_all = select.reshape(3 * rows, total)

    inputs = mm(select_all, tokens_all, 1, 0).astype(BF16).reshape(3, rows, features)
    scaled = (mm(select_all, grads_all, 1, 0) * gate_row.reshape(-1, 1)).astype(BF16)
    scaled = scaled.reshape(3, rows, features)

    gate_w = (w_gate[0], w_gate[1], copy_gate[0])
    up_w = (w_up[0], w_up[1], copy_up[0])
    down_w = (w_down[0], w_down[1], copy_down[0])

    def settle(values):
        if dp_count == 2:
            other = lax.ppermute(values, "dp", [(0, 1), (1, 0)])
            return values.astype(F32) + other.astype(F32)
        return lax.psum(values, "dp").astype(F32)

    def acts_of(s):
        part = jnp.concatenate(
            [
                mm(inputs[s], gate_w[s], 1, 0).astype(BF16),
                mm(inputs[s], up_w[s], 1, 0).astype(BF16),
                mm(scaled[s], down_w[s], 1, 1).astype(BF16),
            ],
            axis=1,
        )
        sums = settle(part)
        return activation(
            sums[:, :width], sums[:, width : 2 * width], sums[:, 2 * width :], served_row[s]
        )

    acts = [None, None, acts_of(2)]
    shadow_acts = lax.all_gather(acts[2], "expert", axis=0, tiled=False)
    acts[0] = acts_of(0)
    acts[1] = acts_of(1)

    route = [
        (
            mm(acts[s][:, :width], gate_w[s], 1, 1)
            + mm(acts[s][:, width : 2 * width], up_w[s], 1, 1)
        ).astype(BF16)
        for s in range(3)
    ]
    route_all = jnp.concatenate(route, axis=0)
    token_part = mm(select_all, route_all, 0, 0).astype(BF16)
    grad_tokens = lax.psum_scatter(token_part, both, scatter_dimension=0, tiled=True)

    out_gate, out_up, out_down = [], [], []
    for s in range(2):
        takes = (shadow_expert == slot_expert[s]).astype(F32)
        whole = acts[s].astype(F32)
        for j in range(expert_count):
            whole = whole + jnp.where(takes[j] > 0, shadow_acts[j].astype(F32), 0.0)
        whole = whole.astype(BF16)
        out_gate.append(mm(inputs[s], whole[:, :width], 0, 0).astype(BF16))
        out_up.append(mm(inputs[s], whole[:, width : 2 * width], 0, 0).astype(BF16))
        out_down.append(mm(whole[:, 2 * width :], scaled[s], 0, 0).astype(BF16))
    return (grad_tokens, jnp.stack(out_gate), jnp.stack(out_up), jnp.stack(out_down))


def solution(mesh):
    return jax.shard_map(
        on_device,
        mesh=mesh,
        in_specs=(
            P(("groups", "expert", "inner"), "dp"),
            P(("groups", "expert", "inner"), "dp"),
            P(("groups", "expert", "inner"), None),
            P(("groups", "expert", "inner"), None),
            P(),
            P("expert", "dp", "inner"),
            P("expert", "dp", "inner"),
            P("expert", "inner", "dp"),
            P("expert", "dp", "inner"),
            P("expert", "dp", "inner"),
            P("expert", "inner", "dp"),
        ),
        out_specs=(
            P(("groups", "expert", "inner"), "dp"),
            P(("groups", "expert"), "dp", "inner"),
            P(("groups", "expert"), "dp", "inner"),
            P(("groups", "expert"), "inner", "dp"),
        ),
        check_vma=False,
    )
```

```python
import jax
import jax.numpy as jnp
from jax import lax
from jax.sharding import PartitionSpec as P

BF16 = jnp.bfloat16
F32 = jnp.float32


def serving_copy(ids, shadow_expert, token_index):
    shadow_count = shadow_expert.shape[0]
    position = token_index[None, :] + jnp.arange(2, dtype=jnp.int32)[:, None]
    matches = (ids[None] == shadow_expert[:, None, None]).astype(jnp.int32)
    copies = 1 + jnp.sum(matches, axis=0)
    chosen = position % copies
    slot_order = jnp.arange(shadow_count, dtype=jnp.int32)
    lower_slot = (slot_order[:, None] > slot_order[None, :]).astype(jnp.int32)
    same_expert = (shadow_expert[:, None] == shadow_expert[None, :]).astype(jnp.int32)
    rank_among = jnp.sum(lower_slot * same_expert, axis=1)
    picked = matches * (rank_among[:, None, None] == chosen[None] - 1).astype(jnp.int32)
    holder = jnp.sum(picked * slot_order[:, None, None], axis=0)
    shadowed = jnp.sum(picked, axis=0)
    return jnp.where(shadowed > 0, 2 * shadow_count + holder, ids)


def activation(pre_gate, pre_up, hidden_grad, served):
    sig = jax.nn.sigmoid(pre_gate)
    swish = pre_gate * sig
    grad_up = hidden_grad * swish
    grad_gate = hidden_grad * pre_up * sig * (1.0 + pre_gate * (1.0 - sig))
    hidden = swish * pre_up
    keep = served[:, None] > 0
    wide = jnp.concatenate([grad_gate, grad_up, hidden], axis=1)
    return jnp.where(keep, wide, 0.0).astype(BF16)


def mm(a, b, ca, cb):
    return lax.dot_general(a, b, (((ca,), (cb,)), ((), ())), preferred_element_type=F32)


def on_device(
    tokens,
    out_grad,
    expert_ids,
    gate_weights,
    shadow_expert,
    w_gate,
    w_up,
    w_down,
    copy_gate,
    copy_up,
    copy_down,
):
    tok_rows, features = tokens.shape
    width = w_gate.shape[2]
    expert_count = lax.axis_size("expert")
    inner_count = lax.axis_size("inner")
    dp_count = lax.axis_size("dp")
    blocks = expert_count * inner_count
    total = blocks * tok_rows
    capacity = max(2, 3 * tok_rows // (2 * expert_count))
    rows = blocks * capacity
    me = lax.axis_index("expert")
    both = ("expert", "inner")

    core = lax.axis_index("inner")
    swap = [(0, 1), (1, 0)]
    meta = jnp.concatenate([expert_ids.astype(F32).T, gate_weights.T], axis=0)
    meta = lax.all_gather(meta, both, axis=0, tiled=False)
    meta = meta.reshape(expert_count, inner_count, 4, tok_rows)
    meta = jnp.where(core == 0, meta, meta[:, ::-1])
    meta = jnp.transpose(meta, (2, 1, 0, 3)).reshape(4, total)
    expert_of = jnp.arange(expert_count, dtype=jnp.int32)[None, :, None]
    core_of = jnp.stack([core, 1 - core]).astype(jnp.int32)[:, None, None]
    token_index = (expert_of * inner_count + core_of) * tok_rows + jnp.arange(
        tok_rows, dtype=jnp.int32
    )
    token_index = token_index.reshape(total)

    def across(near):
        return jnp.concatenate([near, lax.ppermute(near, "inner", swap)], axis=0)

    def after(values, *others):
        return lax.optimization_barrier((values,) + others)[0]

    tokens_all = across(lax.all_gather(tokens, "expert", axis=0, tiled=True))
    grads_near = lax.all_gather(out_grad, "expert", axis=0, tiled=True)

    ids = meta[:2].astype(jnp.int32)
    gates = meta[2:]
    copy_ids = serving_copy(ids, shadow_expert, token_index)
    slot_expert = jnp.stack([2 * me, 2 * me + 1, shadow_expert[me]])
    slot_copy = jnp.stack([2 * me, 2 * me + 1, 2 * expert_count + me])
    member = ids[None] == slot_expert[:, None, None]
    named = jnp.sum(member.astype(F32), axis=1)
    gate_of = jnp.sum(jnp.where(member, gates[None], 0.0), axis=1)
    served_of = jnp.sum((copy_ids[None] == slot_copy[:, None, None]).astype(F32), axis=1)
    before = (jnp.arange(tok_rows)[:, None] < jnp.arange(tok_rows)[None, :]).astype(BF16)
    rank = jnp.dot(
        named.reshape(3 * blocks, tok_rows).astype(BF16), before, preferred_element_type=F32
    ).astype(jnp.int32)
    rank = rank.reshape(3, blocks, tok_rows)
    place = rank + capacity * jnp.arange(blocks, dtype=jnp.int32)[None, :, None]
    place = jnp.where(named > 0, place.reshape(3, total), -1)
    hit = place[:, None, :] == jnp.arange(rows, dtype=jnp.int32)[None, :, None]
    gate_row = jnp.sum(jnp.where(hit, gate_of[:, None, :], 0.0), axis=2)
    served_row = jnp.sum(jnp.where(hit, served_of[:, None, :], 0.0), axis=2)
    select = hit.astype(BF16)
    select_all = select.reshape(3 * rows, total)

    inputs = mm(select_all, tokens_all, 1, 0).astype(BF16).reshape(3, rows, features)
    gate_w = (w_gate[0], w_gate[1], copy_gate[0])
    up_w = (w_up[0], w_up[1], copy_up[0])
    down_w = (w_down[0], w_down[1], copy_down[0])

    def settle(values):
        if dp_count == 2:
            other = lax.ppermute(values, "dp", swap)
            return values.astype(F32) + other.astype(F32)
        return lax.psum(values, "dp").astype(F32)

    def first_of(s):
        return jnp.concatenate(
            [
                mm(inputs[s], gate_w[s], 1, 0).astype(BF16),
                mm(inputs[s], up_w[s], 1, 0).astype(BF16),
            ],
            axis=1,
        )

    def scaled_rows(near):
        values = mm(select_all, across(near), 1, 0) * gate_row.reshape(-1, 1)
        return values.astype(BF16).reshape(3, rows, features)

    def second_of(s):
        return mm(scaled[s], down_w[s], 1, 1).astype(BF16)

    def joined(first, second, served):
        return activation(first[:, :width], first[:, width:], second, served)

    def back(acts, s):
        return (
            mm(acts[:, :width], gate_w[s], 1, 1) + mm(acts[:, width : 2 * width], up_w[s], 1, 1)
        ).astype(BF16)

    takes = [(shadow_expert == slot_expert[s]) for s in range(2)]

    def owners_sum(gathered):
        sums = []
        for s in range(2):
            whole = jnp.zeros(gathered.shape[1:], F32)
            for j in range(expert_count):
                whole = whole + jnp.where(takes[s][j], gathered[j].astype(F32), 0.0)
            sums.append(whole.astype(BF16))
        return jnp.stack(sums)

    first = [first_of(s) for s in range(3)]
    if dp_count == 2:
        half = rows // 2
        side = lax.axis_index("dp")

        def halves(values):
            low, high = values[:half], values[half:]
            return jnp.where(side == 0, low, high), jnp.where(side == 0, high, low)

        def ordered(mine, other, axis):
            low = jnp.where(side == 0, mine, other)
            high = jnp.where(side == 0, other, mine)
            return jnp.concatenate([low, high], axis=axis)

        keep_first, give_first = halves(first[2])
        keep_served = jnp.where(side == 0, served_row[2][:half], served_row[2][half:])
        got_first = lax.ppermute(give_first, "dp", swap)
        scaled = scaled_rows(after(grads_near, got_first))
        keep_second, give_second = halves(second_of(2))
        got_second = lax.ppermute(give_second, "dp", swap)
        first[0] = after(first[0], got_first)
        first[1] = after(first[1], got_second)
        second = [after(second_of(s), got_second) for s in range(2)]
        acts_half = joined(
            keep_first.astype(F32) + got_first.astype(F32),
            keep_second.astype(F32) + got_second.astype(F32),
            keep_served,
        )
        shadow_acts = lax.all_gather(acts_half, "expert", axis=0, tiled=False)
        acts_other = lax.ppermute(acts_half[:, : 2 * width], "dp", swap)
        shadow_back = ordered(back(acts_half, 2), back(acts_other, 2), 0)
        added = owners_sum(shadow_acts)
        added = ordered(added, lax.ppermute(added, "dp", swap), 1)
    else:
        scaled = scaled_rows(grads_near)
        second = [second_of(s) for s in range(3)]
        acts_shadow = joined(settle(first[2]), settle(second[2]), served_row[2])
        shadow_acts = lax.all_gather(acts_shadow, "expert", axis=0, tiled=False)
        shadow_back = back(acts_shadow, 2)
        added = owners_sum(shadow_acts)

    acts = []
    for s in range(2):
        acts.append(joined(settle(first[s]), settle(second[s]), served_row[s]))

    route_all = jnp.concatenate([back(acts[0], 0), back(acts[1], 1), shadow_back], axis=0)
    token_part = mm(select_all, route_all, 0, 0).astype(BF16)
    near, far = token_part[: total // 2], token_part[total // 2 :]
    near = near.astype(F32) + lax.ppermute(far, "inner", swap).astype(F32)
    near = near.astype(BF16)
    if expert_count <= 4:
        near = near.reshape(expert_count, tok_rows, features)
        grad_tokens = lax.dynamic_index_in_dim(near, me, 0, False).astype(F32)
        for step in range(1, expert_count):
            piece = lax.dynamic_index_in_dim(near, (me + step) % expert_count, 0, False)
            ring = [(i, (i + step) % expert_count) for i in range(expert_count)]
            grad_tokens = grad_tokens + lax.ppermute(piece, "expert", ring).astype(F32)
        grad_tokens = grad_tokens.astype(BF16)
    else:
        grad_tokens = lax.psum_scatter(near, "expert", scatter_dimension=0, tiled=True)

    whole = (jnp.stack(acts).astype(F32) + added.astype(F32)).astype(BF16)

    def outer(a, b):
        dims = (((1,), (1,)), ((0,), (0,)))
        return lax.dot_general(a, b, dims, preferred_element_type=F32).astype(BF16)

    return (
        grad_tokens,
        outer(inputs[:2], whole[:, :, :width]),
        outer(inputs[:2], whole[:, :, width : 2 * width]),
        outer(whole[:, :, 2 * width :], scaled[:2]),
    )


def solution(mesh):
    return jax.shard_map(
        on_device,
        mesh=mesh,
        in_specs=(
            P(("groups", "expert", "inner"), "dp"),
            P(("groups", "expert", "inner"), "dp"),
            P(("groups", "expert", "inner"), None),
            P(("groups", "expert", "inner"), None),
            P(),
            P("expert", "dp", "inner"),
            P("expert", "dp", "inner"),
            P("expert", "inner", "dp"),
            P("expert", "dp", "inner"),
            P("expert", "dp", "inner"),
            P("expert", "inner", "dp"),
        ),
        out_specs=(
            P(("groups", "expert", "inner"), "dp"),
            P(("groups", "expert"), "dp", "inner"),
            P(("groups", "expert"), "dp", "inner"),
            P(("groups", "expert"), "inner", "dp"),
        ),
        check_vma=False,
    )
```

```python
import jax
import jax.numpy as jnp
from jax import lax
from jax.sharding import PartitionSpec as P

BF16 = jnp.bfloat16
F32 = jnp.float32


def serving_copy(ids, shadow_expert, token_index):
    shadow_count = shadow_expert.shape[0]
    position = token_index[None, :] + jnp.arange(2, dtype=jnp.int32)[:, None]
    matches = (ids[None] == shadow_expert[:, None, None]).astype(jnp.int32)
    copies = 1 + jnp.sum(matches, axis=0)
    chosen = position % copies
    slot_order = jnp.arange(shadow_count, dtype=jnp.int32)
    lower_slot = (slot_order[:, None] > slot_order[None, :]).astype(jnp.int32)
    same_expert = (shadow_expert[:, None] == shadow_expert[None, :]).astype(jnp.int32)
    rank_among = jnp.sum(lower_slot * same_expert, axis=1)
    picked = matches * (rank_among[:, None, None] == chosen[None] - 1).astype(jnp.int32)
    holder = jnp.sum(picked * slot_order[:, None, None], axis=0)
    shadowed = jnp.sum(picked, axis=0)
    return jnp.where(shadowed > 0, 2 * shadow_count + holder, ids)


def activation(pre_gate, pre_up, hidden_grad, served):
    sig = jax.nn.sigmoid(pre_gate)
    swish = pre_gate * sig
    grad_up = hidden_grad * swish
    grad_gate = hidden_grad * pre_up * sig * (1.0 + pre_gate * (1.0 - sig))
    hidden = swish * pre_up
    keep = served[:, None] > 0
    wide = jnp.concatenate([grad_gate, grad_up, hidden], axis=1)
    return jnp.where(keep, wide, 0.0).astype(BF16)


def mm(a, b, ca, cb):
    return lax.dot_general(a, b, (((ca,), (cb,)), ((), ())), preferred_element_type=F32)


def on_device(
    tokens,
    out_grad,
    expert_ids,
    gate_weights,
    shadow_expert,
    w_gate,
    w_up,
    w_down,
    copy_gate,
    copy_up,
    copy_down,
):
    tok_rows, features = tokens.shape
    width = w_gate.shape[2]
    expert_count = lax.axis_size("expert")
    inner_count = lax.axis_size("inner")
    dp_count = lax.axis_size("dp")
    blocks = expert_count * inner_count
    total = blocks * tok_rows
    capacity = max(2, 3 * tok_rows // (2 * expert_count))
    rows = blocks * capacity
    me = lax.axis_index("expert")
    both = ("expert", "inner")

    core = lax.axis_index("inner")
    swap = [(0, 1), (1, 0)]
    meta = jnp.concatenate([expert_ids.astype(F32).T, gate_weights.T], axis=0)
    meta = lax.all_gather(meta, both, axis=0, tiled=False)
    meta = meta.reshape(expert_count, inner_count, 4, tok_rows)
    meta = jnp.where(core == 0, meta, meta[:, ::-1])
    meta = jnp.transpose(meta, (2, 1, 0, 3)).reshape(4, total)
    expert_of = jnp.arange(expert_count, dtype=jnp.int32)[None, :, None]
    core_of = jnp.stack([core, 1 - core]).astype(jnp.int32)[:, None, None]
    token_index = (expert_of * inner_count + core_of) * tok_rows + jnp.arange(
        tok_rows, dtype=jnp.int32
    )
    token_index = token_index.reshape(total)

    def across(near):
        return jnp.concatenate([near, lax.ppermute(near, "inner", swap)], axis=0)

    def after(values, *others):
        return lax.optimization_barrier((values,) + others)[0]

    tokens_all = across(lax.all_gather(tokens, "expert", axis=0, tiled=True))
    grads_near = lax.all_gather(out_grad, "expert", axis=0, tiled=True)

    ids = meta[:2].astype(jnp.int32)
    gates = meta[2:]
    copy_ids = serving_copy(ids, shadow_expert, token_index)
    slot_expert = jnp.stack([2 * me, 2 * me + 1, shadow_expert[me]])
    slot_copy = jnp.stack([2 * me, 2 * me + 1, 2 * expert_count + me])
    member = ids[None] == slot_expert[:, None, None]
    named = jnp.sum(member.astype(F32), axis=1)
    gate_of = jnp.sum(jnp.where(member, gates[None], 0.0), axis=1)
    served_of = jnp.sum((copy_ids[None] == slot_copy[:, None, None]).astype(F32), axis=1)
    before = (jnp.arange(tok_rows)[:, None] < jnp.arange(tok_rows)[None, :]).astype(BF16)
    rank = jnp.dot(
        named.reshape(3 * blocks, tok_rows).astype(BF16), before, preferred_element_type=F32
    ).astype(jnp.int32)
    rank = rank.reshape(3, blocks, tok_rows)
    place = rank + capacity * jnp.arange(blocks, dtype=jnp.int32)[None, :, None]
    place = jnp.where(named > 0, place.reshape(3, total), -1)
    hit = place[:, None, :] == jnp.arange(rows, dtype=jnp.int32)[None, :, None]
    gate_row = jnp.sum(jnp.where(hit, gate_of[:, None, :], 0.0), axis=2)
    served_row = jnp.sum(jnp.where(hit, served_of[:, None, :], 0.0), axis=2)
    select = hit.astype(BF16)
    select_all = select.reshape(3 * rows, total)

    inputs = mm(select_all, tokens_all, 1, 0).astype(BF16).reshape(3, rows, features)
    gate_w = (w_gate[0], w_gate[1], copy_gate[0])
    up_w = (w_up[0], w_up[1], copy_up[0])
    down_w = (w_down[0], w_down[1], copy_down[0])

    def settle(values):
        if dp_count == 2:
            other = lax.ppermute(values, "dp", swap)
            return values.astype(F32) + other.astype(F32)
        return lax.psum(values, "dp").astype(F32)

    def first_of(s):
        return jnp.concatenate(
            [
                mm(inputs[s], gate_w[s], 1, 0).astype(BF16),
                mm(inputs[s], up_w[s], 1, 0).astype(BF16),
            ],
            axis=1,
        )

    def scaled_rows(near):
        values = mm(select_all, across(near), 1, 0) * gate_row.reshape(-1, 1)
        return values.astype(BF16).reshape(3, rows, features)

    def second_of(s):
        return mm(scaled[s], down_w[s], 1, 1).astype(BF16)

    def joined(first, second, served):
        return activation(first[:, :width], first[:, width:], second, served)

    def back(acts, s):
        return (
            mm(acts[:, :width], gate_w[s], 1, 1) + mm(acts[:, width : 2 * width], up_w[s], 1, 1)
        ).astype(BF16)

    takes = [(shadow_expert == slot_expert[s]) for s in range(2)]

    def owners_sum(gathered):
        sums = []
        for s in range(2):
            whole = jnp.zeros(gathered.shape[1:], BF16)
            for j in range(expert_count):
                whole = whole + jnp.where(takes[s][j], gathered[j], jnp.zeros((), BF16))
            sums.append(whole)
        return jnp.stack(sums)

    first = [first_of(s) for s in range(3)]
    if dp_count == 2:
        half = rows // 2
        side = lax.axis_index("dp")

        def halves(values):
            low, high = values[:half], values[half:]
            return jnp.where(side == 0, low, high), jnp.where(side == 0, high, low)

        def ordered(mine, other, axis):
            low = jnp.where(side == 0, mine, other)
            high = jnp.where(side == 0, other, mine)
            return jnp.concatenate([low, high], axis=axis)

        keep_first, give_first = halves(first[2])
        keep_served = jnp.where(side == 0, served_row[2][:half], served_row[2][half:])
        got_first = lax.ppermute(give_first, "dp", swap)
        scaled = scaled_rows(after(grads_near, got_first))
        keep_second, give_second = halves(second_of(2))
        got_second = lax.ppermute(give_second, "dp", swap)
        first_other = [lax.ppermute(first[0], "dp", swap)]
        first[1] = after(first[1], got_second)
        first_other.append(lax.ppermute(first[1], "dp", swap))
        first_other = [after(values, got_second) for values in first_other]
        first_sum = [first[s].astype(F32) + first_other[s].astype(F32) for s in range(2)]
        second = [after(second_of(s), got_second) for s in range(2)]
        acts_half = joined(
            keep_first.astype(F32) + got_first.astype(F32),
            keep_second.astype(F32) + got_second.astype(F32),
            keep_served,
        )
        shadow_acts = lax.all_gather(acts_half, "expert", axis=0, tiled=False)
        acts_other = lax.ppermute(acts_half[:, : 2 * width], "dp", swap)
        shadow_back = ordered(back(acts_half, 2), back(acts_other, 2), 0)
        added = owners_sum(shadow_acts)
        added = ordered(added, lax.ppermute(added, "dp", swap), 1)
    else:
        scaled = scaled_rows(grads_near)
        second = [second_of(s) for s in range(3)]
        acts_shadow = joined(settle(first[2]), settle(second[2]), served_row[2])
        shadow_acts = lax.all_gather(acts_shadow, "expert", axis=0, tiled=False)
        first_sum = [settle(first[s]) for s in range(2)]
        shadow_back = back(acts_shadow, 2)
        added = owners_sum(shadow_acts)

    acts = []
    for s in range(2):
        acts.append(joined(first_sum[s], settle(second[s]), served_row[s]))

    route_all = jnp.concatenate([back(acts[0], 0), back(acts[1], 1), shadow_back], axis=0)
    token_part = mm(select_all, route_all, 0, 0).astype(BF16)
    near, far = token_part[: total // 2], token_part[total // 2 :]
    near = near.astype(F32) + lax.ppermute(far, "inner", swap).astype(F32)
    near = near.astype(BF16)
    if expert_count <= 4:
        near = near.reshape(expert_count, tok_rows, features)
        grad_tokens = lax.dynamic_index_in_dim(near, me, 0, False).astype(F32)
        for step in range(1, expert_count):
            piece = lax.dynamic_index_in_dim(near, (me + step) % expert_count, 0, False)
            ring = [(i, (i + step) % expert_count) for i in range(expert_count)]
            grad_tokens = grad_tokens + lax.ppermute(piece, "expert", ring).astype(F32)
        grad_tokens = grad_tokens.astype(BF16)
    else:
        grad_tokens = lax.psum_scatter(near, "expert", scatter_dimension=0, tiled=True)

    whole = (jnp.stack(acts).astype(F32) + added.astype(F32)).astype(BF16)

    def outer(a, b):
        dims = (((1,), (1,)), ((0,), (0,)))
        return lax.dot_general(a, b, dims, preferred_element_type=F32).astype(BF16)

    return (
        grad_tokens,
        outer(inputs[:2], whole[:, :, :width]),
        outer(inputs[:2], whole[:, :, width : 2 * width]),
        outer(whole[:, :, 2 * width :], scaled[:2]),
    )


def solution(mesh):
    return jax.shard_map(
        on_device,
        mesh=mesh,
        in_specs=(
            P(("groups", "expert", "inner"), "dp"),
            P(("groups", "expert", "inner"), "dp"),
            P(("groups", "expert", "inner"), None),
            P(("groups", "expert", "inner"), None),
            P(),
            P("expert", "dp", "inner"),
            P("expert", "dp", "inner"),
            P("expert", "inner", "dp"),
            P("expert", "dp", "inner"),
            P("expert", "dp", "inner"),
            P("expert", "inner", "dp"),
        ),
        out_specs=(
            P(("groups", "expert", "inner"), "dp"),
            P(("groups", "expert"), "dp", "inner"),
            P(("groups", "expert"), "dp", "inner"),
            P(("groups", "expert"), "inner", "dp"),
        ),
        check_vma=False,
    )
```
